32 devices in a mesh: ctx: 8 (over z, x), tp: 4 (over y, core).
Axes of the slice: x: 2, y: 2, z: 4, core: 2. Of those that a mesh axis runs over, the one named last changes fastest.
Arguments:
- queries: bfloat16 [2048, 2560], P('ctx', 'tp'), may hold values from -5 to 5
- keys: bfloat16 [2048, 2560], P('ctx', 'tp'), may hold values from -5 to 5
- values: bfloat16 [2048, 2560], P('ctx', 'tp'), may hold values from -6 to 6
- block_mask: int32 [16, 16], replicated, may hold values from 0 to 1, as said below
- w_out: bfloat16 [2560, 5120], P('tp'), may hold values from -0.125 to 0.125
Outputs:
- mixed: bfloat16 [2048, 5120], P('ctx', 'tp')
The draws below stay inside these ranges and needn't reach their ends.
Inputs may be any that keep to these rules, and one draw needn't show every extreme that they name: block_mask[b, b] = 1 for every block b. block_mask[i, j] = 0 whenever the ctx indices i // 2 and j // 2 differ by more than 2; where they differ by exactly 2 and i and j have the same position within their devices, block_mask[i, j] = 1.
All inputs are finite; a program needn't handle non-finite values.
Results may differ from the reference program's by a relative error of at most 0.014.
Values may be sent and summed in bfloat16 or wider, within the bound.
A program may use at most 64 MiB of HBM per device.

```python
import jax
import jax.numpy as jnp
from jax import lax

D = 5120
HEADS = 20
HD = 128
BLK = 128
TOK_DEV = 256
TOKENS = 2048
NB = 16
REACH = 2


def query_key_pair(key):
    base = jax.random.fold_in(key, 7)
    key_query, key_key = jax.random.split(base, 2)
    shape = (TOKENS, HEADS * HD)
    query_draw = jax.random.normal(key_query, shape, jnp.float32)
    key_draw = jax.random.normal(key_key, shape, jnp.float32)
    return (jnp.clip(query_draw, -5.0, 5.0), jnp.clip(key_draw, -5.0, 5.0))


def draw_queries(key, part):
    return query_key_pair(key)[0].astype(jnp.bfloat16)


def draw_keys(key, part):
    return query_key_pair(key)[1].astype(jnp.bfloat16)


def draw_block_mask(key, part):
    per_dev = TOK_DEV // BLK
    row_ids = jnp.arange(NB, dtype=jnp.int32)[:, None]
    col_ids = jnp.arange(NB, dtype=jnp.int32)[None, :]
    distance = jnp.abs(row_ids // per_dev - col_ids // per_dev)
    chance = jax.random.randint(jax.random.fold_in(key, 11), (NB, NB), 0, 1000)
    keep = (chance < 900 // (1 + distance)) & (distance <= REACH)
    forced = (distance == REACH) & (row_ids % per_dev == col_ids % per_dev)
    keep = keep | (row_ids == col_ids) | forced
    return keep.astype(jnp.int32)


def levels(own_key, extent, cuts, low, top_value):
    factor_of = 1.0
    for position, blocks in cuts:
        steps = jax.random.uniform(jax.random.fold_in(jax.random.fold_in(own_key, 6), position), (blocks,), jnp.float32, low / len(cuts), top_value / len(cuts))
        factor_of = factor_of * jnp.repeat(jnp.exp(steps), extent[position] // blocks).reshape((-1,) + (1,) * (len(extent) - 1 - position))
    return factor_of


def bell_draw(own_key, extent, scale, bound, cuts=(), held_as=jnp.bfloat16):
    drawn = scale * jax.random.normal(own_key, extent, jnp.float32)
    if cuts:
        drawn = drawn * levels(own_key, extent, cuts, -0.22, 0.18)
    return jnp.clip(drawn, -bound, bound).astype(held_as)


def setup_inputs(seed: int = 0) -> dict:
    streams_of = jax.random.split(jax.random.key(seed), 6)
    queries = draw_queries(jax.random.fold_in(streams_of[5], 71), 0)
    keys = draw_keys(jax.random.fold_in(streams_of[5], 71), 0)
    values = bell_draw(streams_of[2], (TOKENS, HEADS * HD), 1.0, 6.0, ((0, 8), (1, 4)))
    block_mask = draw_block_mask(jax.random.fold_in(streams_of[5], 71), 0)
    w_out = bell_draw(streams_of[4], (HEADS * HD, D), (HEADS * HD) ** -0.5, 0.125, ((0, 4),))
    return {"queries": queries, "keys": keys, "values": values, "block_mask": block_mask, "w_out": w_out}


def reference(queries, keys, values, block_mask, w_out):
    scale = HD ** -0.5
    allowed = jnp.repeat(jnp.repeat(block_mask, BLK, axis=0), BLK, axis=1) > 0
    query_heads = queries.reshape(TOKENS, HEADS, HD)
    key_heads = keys.reshape(TOKENS, HEADS, HD)
    value_heads = values.reshape(TOKENS, HEADS, HD)

    def one_head(head):
        query_one = lax.dynamic_index_in_dim(query_heads, head, 1, keepdims=False)
        key_one = lax.dynamic_index_in_dim(key_heads, head, 1, keepdims=False)
        value_one = lax.dynamic_index_in_dim(value_heads, head, 1, keepdims=False)
        scores = jnp.dot(query_one, key_one.T, preferred_element_type=jnp.float32) * scale
        masked = jnp.where(allowed, scores, jnp.float32(-1e30))
        maxima = jnp.max(masked, axis=1, keepdims=True)
        probs = jnp.where(allowed, jnp.exp(masked - maxima), jnp.float32(0.0))
        totals = jnp.sum(probs, axis=1, keepdims=True)
        summed = jnp.dot(probs.astype(jnp.bfloat16), value_one, preferred_element_type=jnp.float32)
        return summed / totals

    outputs = lax.map(one_head, jnp.arange(HEADS, dtype=jnp.int32))
    attended = jnp.transpose(outputs, (1, 0, 2)).reshape(TOKENS, HEADS * HD).astype(jnp.bfloat16)
    return jnp.dot(attended, w_out, preferred_element_type=jnp.float32).astype(jnp.bfloat16)
```

```python
import functools
import math

import jax
import jax.numpy as jnp
from jax import lax
from jax.experimental import pallas as pl
from jax.experimental.pallas import tpu as pltpu
from jax.sharding import PartitionSpec as P

HD = 128
BLK = 128
MESH = pl.DeviceIdType.MESH
K, V = 0, 1


def kernel(
    reach, count, tp_count, chunks,
    mask_ref, q_ref, k_ref, v_ref, w_ref, out_ref,
    kv, w_vm, acc, peak, total, att, stage_p, recv_p, stage_y, recv_y, final,
    kv_local, w_local, own_send, relay_send, kv_recv, p_send, p_recv, y_send, y_recv,
):
    tok, cols = q_ref.shape
    heads = cols // HD
    per = tok // BLK
    chips = tp_count // 2
    out_cols = out_ref.shape[1]
    width = out_cols // chunks
    ctx = lax.axis_index("ctx")
    t = lax.axis_index("tp")
    inner = lax.rem(ctx, reach)
    core = lax.rem(t, 2)
    chip = t // 2
    partner = chip * 2 + 1 - core

    def tp_of(jy, which):
        return lax.rem(chip + jy, chips) * 2 + which

    def each_peer(fn):
        if reach == 2:
            fn(1)
        elif reach > 2:
            def step(j, carry):
                fn(j)
                return carry
            lax.fori_loop(1, reach, step, 0)

    def row_peer(j):
        return ctx - inner + lax.rem(inner + j, reach)

    def inside(c):
        return jnp.logical_and(c >= 0, c < count)

    own = [
        pltpu.make_async_copy(k_ref, kv.at[reach, K], kv_local.at[K]),
        pltpu.make_async_copy(v_ref, kv.at[reach, V], kv_local.at[V]),
    ]
    weights = [
        pltpu.make_async_copy(
            w_ref.at[:, s * out_cols:(s + 1) * out_cols], w_vm.at[s], w_local.at[s]
        )
        for s in range(tp_count)
    ]
    for copy in own:
        copy.start()

    barrier = pltpu.get_barrier_semaphore()

    def greet(c, tt):
        pl.semaphore_signal(barrier, inc=1, device_id=(c, tt), device_id_type=MESH)

    each_peer(lambda j: greet(row_peer(j), t))
    for away in (-reach, reach):
        @pl.when(inside(ctx + away))
        def _(away=away):
            greet(ctx + away, t)
    greet(ctx, partner)
    for jy in range(1, chips):
        greet(ctx, tp_of(jy, core))
    outer_count = inside(ctx - reach).astype(jnp.int32) + inside(ctx + reach).astype(jnp.int32)
    pl.semaphore_wait(barrier, reach - 1 + 1 + chips - 1 + outer_count)

    def own_copy(dest, half):
        return pltpu.make_async_remote_copy(
            src_ref=(k_ref, v_ref)[half],
            dst_ref=kv.at[ctx - dest + reach, half],
            send_sem=own_send.at[dest - ctx + reach, half],
            recv_sem=kv_recv.at[ctx - dest + reach, half],
            device_id=(dest, t),
            device_id_type=MESH,
        )

    def outer(fn):
        for away in (-reach, reach):
            @pl.when(inside(ctx + away))
            def _(away=away):
                fn(ctx + away)

    each_peer(lambda j: own_copy(row_peer(j), V).start())
    outer(lambda dest: own_copy(dest, K).start())
    each_peer(lambda j: own_copy(row_peer(j), K).start())
    outer(lambda dest: own_copy(dest, V).start())
    for copy in weights:
        copy.start()

    def wait_piece(src, half):
        slot = src - ctx + reach
        pltpu.make_async_remote_copy(
            src_ref=kv.at[slot, half],
            dst_ref=kv.at[slot, half],
            send_sem=own_send.at[slot, half],
            recv_sem=kv_recv.at[slot, half],
            device_id=(ctx, partner),
            device_id_type=MESH,
        ).wait_recv()

    def attend(src, first):
        slot = src - ctx + reach
        factor = jnp.float32(HD ** (-0.5) * math.log2(math.e))
        bias_rows = []
        for a in range(per):
            parts = []
            for b in range(per):
                flag = mask_ref[ctx * per + a, src * per + b]
                value = jnp.where(flag > 0, jnp.float32(0.0), jnp.float32(-1e30))
                parts.append(jnp.full((1, BLK), value, jnp.float32))
            bias_rows.append(jnp.concatenate(parts, axis=1))
        for h in range(heads):
            lanes = slice(h * HD, (h + 1) * HD)
            key = kv[slot, K, :, lanes]
            value = kv[slot, V, :, lanes]
            for a in range(per):
                rows = slice(a * BLK, (a + 1) * BLK)
                scores = lax.dot_general(
                    q_ref[rows, lanes], key, (((1,), (1,)), ((), ())),
                    preferred_element_type=jnp.float32,
                ) + bias_rows[a]
                top = jnp.max(scores, axis=1, keepdims=True)
                if not first:
                    before = peak[h, rows, 0:1]
                    top = jnp.maximum(before, top)
                weight = jnp.exp2((scores - top) * factor)
                summed = jnp.sum(weight, axis=1, keepdims=True)
                product = jnp.dot(
                    weight.astype(jnp.bfloat16), value, preferred_element_type=jnp.float32
                )
                if not first:
                    fade = jnp.exp2((before - top) * factor)
                    summed = summed + total[h, rows, 0:1] * fade
                    product = product + acc[rows, lanes] * fade
                peak[h, rows, :] = jnp.broadcast_to(top, (BLK, HD))
                total[h, rows, :] = jnp.broadcast_to(summed, (BLK, HD))
                acc[rows, lanes] = product

    for copy in own:
        copy.wait()
    attend(ctx, True)

    def value_relay(j):
        peer = row_peer(j)
        dest = jnp.where(peer > ctx, ctx + reach, ctx - reach)
        copy = pltpu.make_async_remote_copy(
            src_ref=kv.at[peer - ctx + reach, V],
            dst_ref=kv.at[peer - dest + reach, V],
            send_sem=relay_send.at[peer - ctx + reach, V],
            recv_sem=kv_recv.at[peer - dest + reach, V],
            device_id=(dest, t),
            device_id_type=MESH,
        )
        return inside(dest), copy

    def key_relay(j):
        peer = row_peer(j)
        src = jnp.where(peer < ctx, ctx - reach, ctx + reach)
        copy = pltpu.make_async_remote_copy(
            src_ref=kv.at[src - ctx + reach, K],
            dst_ref=kv.at[src - peer + reach, K],
            send_sem=relay_send.at[peer - ctx + reach, K],
            recv_sem=kv_recv.at[src - peer + reach, K],
            device_id=(peer, t),
            device_id_type=MESH,
        )
        return inside(src), copy

    def start_relay(make, j):
        valid, copy = make(j)

        @pl.when(valid)
        def _():
            copy.start()

    def end_relay(make, j):
        valid, copy = make(j)

        @pl.when(valid)
        def _():
            copy.wait_send()

    def take_values(j):
        wait_piece(row_peer(j), V)
        start_relay(value_relay, j)

    each_peer(take_values)
    outer(lambda src: wait_piece(src, K))
    each_peer(lambda j: start_relay(key_relay, j))

    def take_row(j):
        wait_piece(row_peer(j), K)
        attend(row_peer(j), False)

    each_peer(take_row)

    def take_outer(src):
        wait_piece(src, V)
        attend(src, False)

    outer(take_outer)

    def take_diagonal(j):
        peer = row_peer(j)
        src = jnp.where(peer > ctx, peer - reach, peer + reach)

        @pl.when(inside(src))
        def _():
            wait_piece(src, K)
            wait_piece(src, V)
            attend(src, False)

    each_peer(take_diagonal)

    for h in range(heads):
        lanes = slice(h * HD, (h + 1) * HD)
        att[:, lanes] = (acc[:, lanes] * (1.0 / total[h])).astype(jnp.bfloat16)
    for copy in weights:
        copy.wait()

    def project(slab, k):
        return jnp.dot(
            att[...], w_vm[slab, :, k * width:(k + 1) * width],
            preferred_element_type=jnp.float32,
        )

    def partner_copy(jy, k):
        return pltpu.make_async_remote_copy(
            src_ref=stage_p.at[jy, k],
            dst_ref=recv_p.at[jy, k],
            send_sem=p_send.at[jy, k],
            recv_sem=p_recv.at[jy, k],
            device_id=(ctx, partner),
            device_id_type=MESH,
        )

    def chip_copy(jy, k):
        return pltpu.make_async_remote_copy(
            src_ref=stage_y.at[jy, k],
            dst_ref=recv_y.at[chips - jy, k],
            send_sem=y_send.at[jy, k],
            recv_sem=y_recv.at[chips - jy, k],
            device_id=(ctx, tp_of(jy, core)),
            device_id_type=MESH,
        )

    pending = []

    def push(copy):
        while pending:
            pending.pop().start()
        if copy is not None:
            pending.append(copy)

    for jy in range(1, chips):
        for k in range(chunks):
            stage_p[jy, k] = project(tp_of(jy, 1 - core), k).astype(jnp.bfloat16)
            push(partner_copy(jy, k))
    for jy in range(1, chips):
        for k in range(chunks):
            mine = project(tp_of(jy, core), k)
            push(None)
            partner_copy(jy, k).wait_recv()
            stage_y[jy, k] = (mine + recv_p[jy, k].astype(jnp.float32)).astype(jnp.bfloat16)
            push(chip_copy(jy, k))
    for k in range(chunks):
        stage_p[0, k] = project(tp_of(0, 1 - core), k).astype(jnp.bfloat16)
        push(partner_copy(0, k))
    for k in range(chunks):
        mine = project(tp_of(0, core), k)
        push(None)
        partner_copy(0, k).wait_recv()
        final[k] = mine + recv_p[0, k].astype(jnp.float32)
    for k in range(chunks):
        result = final[k]
        for jy in range(1, chips):
            chip_copy(chips - jy, k).wait_recv()
            result = result + recv_y[jy, k].astype(jnp.float32)
        out_ref[:, k * width:(k + 1) * width] = result.astype(jnp.bfloat16)

    each_peer(lambda j: own_copy(row_peer(j), V).wait_send())
    each_peer(lambda j: own_copy(row_peer(j), K).wait_send())
    outer(lambda dest: own_copy(dest, K).wait_send())
    outer(lambda dest: own_copy(dest, V).wait_send())
    each_peer(lambda j: end_relay(value_relay, j))
    each_peer(lambda j: end_relay(key_relay, j))
    for jy in range(chips):
        for k in range(chunks):
            partner_copy(jy, k).wait_send()
    for jy in range(1, chips):
        for k in range(chunks):
            chip_copy(jy, k).wait_send()


def shards(count, tp_count, queries, keys, values, block_mask, w_out):
    tok, cols = queries.shape
    heads = cols // HD
    reach = count // 4
    chips = tp_count // 2
    depth, wide = w_out.shape
    out_cols = wide // tp_count
    chunks = max(1, out_cols // 256)
    width = out_cols // chunks
    bf16, f32 = jnp.bfloat16, jnp.float32
    dma = pltpu.SemaphoreType.DMA
    slots = 2 * reach + 1
    return pl.pallas_call(
        functools.partial(kernel, reach, count, tp_count, chunks),
        out_shape=jax.ShapeDtypeStruct((tok, out_cols), bf16),
        in_specs=[
            pl.BlockSpec(memory_space=pltpu.SMEM),
            pl.BlockSpec(memory_space=pltpu.VMEM),
            pl.BlockSpec(memory_space=pl.ANY),
            pl.BlockSpec(memory_space=pl.ANY),
            pl.BlockSpec(memory_space=pl.ANY),
        ],
        out_specs=pl.BlockSpec(memory_space=pltpu.VMEM),
        scratch_shapes=[
            pltpu.VMEM((slots, 2, tok, cols), bf16),
            pltpu.VMEM((tp_count, depth, out_cols), bf16),
            pltpu.VMEM((tok, cols), f32),
            pltpu.VMEM((heads, tok, HD), f32),
            pltpu.VMEM((heads, tok, HD), f32),
            pltpu.VMEM((tok, cols), bf16),
            pltpu.VMEM((chips, chunks, tok, width), bf16),
            pltpu.VMEM((chips, chunks, tok, width), bf16),
            pltpu.VMEM((chips, chunks, tok, width), bf16),
            pltpu.VMEM((chips, chunks, tok, width), bf16),
            pltpu.VMEM((chunks, tok, width), f32),
            dma((2,)),
            dma((tp_count,)),
            dma((slots, 2)),
            dma((slots, 2)),
            dma((slots, 2)),
            dma((chips, chunks)),
            dma((chips, chunks)),
            dma((chips, chunks)),
            dma((chips, chunks)),
        ],
        compiler_params=pltpu.CompilerParams(
            collective_id=0, has_side_effects=True, vmem_limit_bytes=60 * 1024 * 1024
        ),
    )(block_mask, queries, keys, values, w_out)


def solution(mesh):
    return jax.shard_map(
        functools.partial(shards, mesh.shape["ctx"], mesh.shape["tp"]),
        mesh=mesh,
        in_specs=(P("ctx", "tp"), P("ctx", "tp"), P("ctx", "tp"), P(), P("tp", None)),
        out_specs=P("ctx", "tp"),
        check_vma=False,
    )
```

```python
import functools
import math

import jax
import jax.numpy as jnp
from jax import lax
from jax.experimental import pallas as pl
from jax.experimental.pallas import tpu as pltpu
from jax.sharding import PartitionSpec as P

HD = 128
BLK = 128
MESH = pl.DeviceIdType.MESH
K, V = 0, 1
OUTER_FIRST, ROW_FIRST = 0, 1


def kernel(
    reach, count, tp_count, chunks,
    mask_ref, q_ref, k_ref, v_ref, w_ref, out_ref,
    kv, w_vm, acc, peak, att, stage_p, recv_p, stage_y, recv_y, final,
    kv_local, w_local, own_send, relay_send, kv_recv, p_send, p_recv, y_send, y_recv,
):
    tok, cols = q_ref.shape
    heads = cols // HD
    per = tok // BLK
    chips = tp_count // 2
    out_cols = out_ref.shape[1]
    width = out_cols // chunks
    ctx = lax.axis_index("ctx")
    t = lax.axis_index("tp")
    inner = lax.rem(ctx, reach)
    core = lax.rem(t, 2)
    chip = t // 2
    partner = chip * 2 + 1 - core

    def tp_of(jy, which):
        return lax.rem(chip + jy, chips) * 2 + which

    def each_peer(fn):
        if reach == 2:
            fn(1)
        elif reach > 2:
            def step(j, carry):
                fn(j)
                return carry
            lax.fori_loop(1, reach, step, 0)

    def row_peer(j):
        return ctx - inner + lax.rem(inner + j, reach)

    def inside(c):
        return jnp.logical_and(c >= 0, c < count)

    part_rows = tok // 2

    def part_of(half, kind):
        return (k_ref, v_ref)[kind].at[half * part_rows:(half + 1) * part_rows, :]

    own = [
        pltpu.make_async_copy(
            part_of(half, kind), kv.at[reach, half * 2 + kind], kv_local.at[half * 2 + kind]
        )
        for half in (0, 1) for kind in (K, V)
    ]
    weights = [
        pltpu.make_async_copy(
            w_ref.at[:, s * out_cols:(s + 1) * out_cols], w_vm.at[s], w_local.at[s]
        )
        for s in range(tp_count)
    ]
    for copy in own:
        copy.start()

    barrier = pltpu.get_barrier_semaphore()

    def greet(c, tt):
        pl.semaphore_signal(barrier, inc=1, device_id=(c, tt), device_id_type=MESH)

    each_peer(lambda j: greet(row_peer(j), t))
    for away in (-reach, reach):
        @pl.when(inside(ctx + away))
        def _(away=away):
            greet(ctx + away, t)
    greet(ctx, partner)
    for jy in range(1, chips):
        greet(ctx, tp_of(jy, core))
    outer_count = inside(ctx - reach).astype(jnp.int32) + inside(ctx + reach).astype(jnp.int32)
    pl.semaphore_wait(barrier, reach - 1 + 1 + chips - 1 + outer_count)

    class Pair:
        def __init__(self, make):
            self.copies = [make(K), make(V)]

        def start(self):
            for copy in self.copies:
                copy.start()

        def wait_send(self):
            for copy in self.copies:
                copy.wait_send()

        def wait_recv(self):
            for copy in self.copies:
                copy.wait_recv()

    def own_copy(dest, half):
        return Pair(lambda kind: pltpu.make_async_remote_copy(
            src_ref=part_of(half, kind),
            dst_ref=kv.at[ctx - dest + reach, half * 2 + kind],
            send_sem=own_send.at[dest - ctx + reach, half * 2 + kind],
            recv_sem=kv_recv.at[ctx - dest + reach, half * 2 + kind],
            device_id=(dest, t),
            device_id_type=MESH,
        ))

    def outer(fn):
        for away in (-reach, reach):
            @pl.when(inside(ctx + away))
            def _(away=away):
                fn(ctx + away)

    each_peer(lambda j: own_copy(row_peer(j), ROW_FIRST).start())
    outer(lambda dest: own_copy(dest, OUTER_FIRST).start())
    each_peer(lambda j: own_copy(row_peer(j), OUTER_FIRST).start())
    outer(lambda dest: own_copy(dest, ROW_FIRST).start())
    for copy in weights:
        copy.start()

    def wait_piece(src, half):
        slot = src - ctx + reach
        Pair(lambda kind: pltpu.make_async_remote_copy(
            src_ref=kv.at[slot, half * 2 + kind],
            dst_ref=kv.at[slot, half * 2 + kind],
            send_sem=own_send.at[slot, half * 2 + kind],
            recv_sem=kv_recv.at[slot, half * 2 + kind],
            device_id=(ctx, partner),
            device_id_type=MESH,
        )).wait_recv()

    def attend(src, halves, first=False):
        slot = src - ctx + reach
        factor = jnp.float32(HD ** (-0.5) * math.log2(math.e))
        half_blocks = per // 2
        blocks = [half * half_blocks + b for half in halves for b in range(half_blocks)]
        span = len(blocks) * BLK
        bias_rows = []
        for a in range(per):
            parts = []
            for b in blocks:
                flag = mask_ref[ctx * per + a, src * per + b]
                value = jnp.where(flag > 0, jnp.float32(0.0), jnp.float32(-1e30))
                parts.append(jnp.full((1, BLK), value, jnp.float32))
            bias_rows.append(jnp.concatenate(parts, axis=1))
        ones = jnp.ones((span, HD), jnp.bfloat16)
        for h in range(heads):
            lanes = slice(h * HD, (h + 1) * HD)
            key = jnp.concatenate([kv[slot, half * 2 + K, :, lanes] for half in halves], axis=0)
            value = jnp.concatenate([kv[slot, half * 2 + V, :, lanes] for half in halves], axis=0)
            raw = lax.dot_general(
                q_ref[:, lanes], key, (((1,), (1,)), ((), ())),
                preferred_element_type=jnp.float32,
            )
            weights_of, fades = [], []
            for a in range(per):
                rows = slice(a * BLK, (a + 1) * BLK)
                scores = raw[rows] + bias_rows[a]
                top = jnp.broadcast_to(jnp.max(scores, axis=1, keepdims=True), (BLK, HD))
                if not first:
                    before = peak[h, rows, :]
                    top = jnp.maximum(before, top)
                    fades.append(jnp.exp2((before - top) * factor))
                peak[h, rows, :] = top
                wide_top = jnp.concatenate([top] * len(blocks), axis=1)
                weights_of.append(jnp.exp2((scores - wide_top) * factor).astype(jnp.bfloat16))
            product = jnp.dot(
                jnp.concatenate(weights_of, axis=0),
                jnp.concatenate([value, ones], axis=1),
                preferred_element_type=jnp.float32,
            )
            if not first:
                fade = jnp.concatenate(fades, axis=0)
                product = product + acc[h] * jnp.concatenate([fade, fade], axis=1)
            acc[h] = product

    for copy in own:
        copy.wait()
    attend(ctx, (0, 1), True)

    def row_first_relay(j):
        peer = row_peer(j)
        dest = jnp.where(peer > ctx, ctx + reach, ctx - reach)
        return inside(dest), Pair(lambda kind: pltpu.make_async_remote_copy(
            src_ref=kv.at[peer - ctx + reach, ROW_FIRST * 2 + kind],
            dst_ref=kv.at[peer - dest + reach, ROW_FIRST * 2 + kind],
            send_sem=relay_send.at[peer - ctx + reach, ROW_FIRST * 2 + kind],
            recv_sem=kv_recv.at[peer - dest + reach, ROW_FIRST * 2 + kind],
            device_id=(dest, t),
            device_id_type=MESH,
        ))

    def outer_first_relay(j):
        peer = row_peer(j)
        src = jnp.where(peer < ctx, ctx - reach, ctx + reach)
        return inside(src), Pair(lambda kind: pltpu.make_async_remote_copy(
            src_ref=kv.at[src - ctx + reach, OUTER_FIRST * 2 + kind],
            dst_ref=kv.at[src - peer + reach, OUTER_FIRST * 2 + kind],
            send_sem=relay_send.at[peer - ctx + reach, OUTER_FIRST * 2 + kind],
            recv_sem=kv_recv.at[src - peer + reach, OUTER_FIRST * 2 + kind],
            device_id=(peer, t),
            device_id_type=MESH,
        ))

    def start_relay(make, j):
        valid, copy = make(j)

        @pl.when(valid)
        def _():
            copy.start()

    def end_relay(make, j):
        valid, copy = make(j)

        @pl.when(valid)
        def _():
            copy.wait_send()

    def pass_row(j):
        wait_piece(row_peer(j), ROW_FIRST)
        start_relay(row_first_relay, j)

    each_peer(pass_row)
    outer(lambda src: wait_piece(src, OUTER_FIRST))
    each_peer(lambda j: start_relay(outer_first_relay, j))
    each_peer(lambda j: attend(row_peer(j), (ROW_FIRST,)))
    outer(lambda src: attend(src, (OUTER_FIRST,)))

    def take_row(j):
        wait_piece(row_peer(j), OUTER_FIRST)
        attend(row_peer(j), (OUTER_FIRST,))

    each_peer(take_row)

    def take_outer(src):
        wait_piece(src, ROW_FIRST)
        attend(src, (ROW_FIRST,))

    outer(take_outer)
    for copy in weights:
        copy.wait()

    def take_diagonal(j):
        peer = row_peer(j)
        src = jnp.where(peer > ctx, peer - reach, peer + reach)

        @pl.when(inside(src))
        def _():
            wait_piece(src, OUTER_FIRST)
            wait_piece(src, ROW_FIRST)
            attend(src, (0, 1))

    each_peer(take_diagonal)

    for h in range(heads):
        lanes = slice(h * HD, (h + 1) * HD)
        att[:, lanes] = (acc[h, :, :HD] * (1.0 / acc[h, :, HD:])).astype(jnp.bfloat16)

    def project(slab, k):
        return jnp.dot(
            att[...], w_vm[slab, :, k * width:(k + 1) * width],
            preferred_element_type=jnp.float32,
        )

    def partner_copy(jy, k):
        return pltpu.make_async_remote_copy(
            src_ref=stage_p.at[jy, k],
            dst_ref=recv_p.at[jy, k],
            send_sem=p_send.at[jy, k],
            recv_sem=p_recv.at[jy, k],
            device_id=(ctx, partner),
            device_id_type=MESH,
        )

    def chip_copy(jy, k):
        return pltpu.make_async_remote_copy(
            src_ref=stage_y.at[jy, k],
            dst_ref=recv_y.at[chips - jy, k],
            send_sem=y_send.at[jy, k],
            recv_sem=y_recv.at[chips - jy, k],
            device_id=(ctx, tp_of(jy, core)),
            device_id_type=MESH,
        )

    pending = []

    def push(copy):
        while pending:
            pending.pop().start()
        if copy is not None:
            pending.append(copy)

    for jy in range(1, chips):
        for k in range(chunks):
            stage_p[jy, k] = project(tp_of(jy, 1 - core), k).astype(jnp.bfloat16)
            push(partner_copy(jy, k))
    for jy in range(1, chips):
        for k in range(chunks):
            mine = project(tp_of(jy, core), k)
            push(None)
            partner_copy(jy, k).wait_recv()
            stage_y[jy, k] = (mine + recv_p[jy, k].astype(jnp.float32)).astype(jnp.bfloat16)
            push(chip_copy(jy, k))
    for k in range(chunks):
        stage_p[0, k] = project(tp_of(0, 1 - core), k).astype(jnp.bfloat16)
        push(partner_copy(0, k))
    for k in range(chunks):
        mine = project(tp_of(0, core), k)
        push(None)
        partner_copy(0, k).wait_recv()
        final[k] = mine + recv_p[0, k].astype(jnp.float32)
    for k in range(chunks):
        result = final[k]
        for jy in range(1, chips):
            chip_copy(chips - jy, k).wait_recv()
            result = result + recv_y[jy, k].astype(jnp.float32)
        out_ref[:, k * width:(k + 1) * width] = result.astype(jnp.bfloat16)

    each_peer(lambda j: own_copy(row_peer(j), ROW_FIRST).wait_send())
    each_peer(lambda j: own_copy(row_peer(j), OUTER_FIRST).wait_send())
    outer(lambda dest: own_copy(dest, OUTER_FIRST).wait_send())
    outer(lambda dest: own_copy(dest, ROW_FIRST).wait_send())
    each_peer(lambda j: end_relay(row_first_relay, j))
    each_peer(lambda j: end_relay(outer_first_relay, j))
    for jy in range(chips):
        for k in range(chunks):
            partner_copy(jy, k).wait_send()
    for jy in range(1, chips):
        for k in range(chunks):
            chip_copy(jy, k).wait_send()


def shards(count, tp_count, queries, keys, values, block_mask, w_out):
    tok, cols = queries.shape
    heads = cols // HD
    reach = count // 4
    chips = tp_count // 2
    depth, wide = w_out.shape
    out_cols = wide // tp_count
    chunks = max(1, out_cols // 256)
    width = out_cols // chunks
    bf16, f32 = jnp.bfloat16, jnp.float32
    dma = pltpu.SemaphoreType.DMA
    slots = 2 * reach + 1
    held = 2 * (slots * 2 * tok * cols + tp_count * depth * out_cols + 4 * tok * out_cols * chips)
    held += 4 * tok * (5 * cols + 3 * out_cols)
    return pl.pallas_call(
        functools.partial(kernel, reach, count, tp_count, chunks),
        out_shape=jax.ShapeDtypeStruct((tok, out_cols), bf16),
        in_specs=[
            pl.BlockSpec(memory_space=pltpu.SMEM),
            pl.BlockSpec(memory_space=pltpu.VMEM),
            pl.BlockSpec(memory_space=pl.ANY),
            pl.BlockSpec(memory_space=pl.ANY),
            pl.BlockSpec(memory_space=pl.ANY),
        ],
        out_specs=pl.BlockSpec(memory_space=pltpu.VMEM),
        scratch_shapes=[
            pltpu.VMEM((slots, 4, tok // 2, cols), bf16),
            pltpu.VMEM((tp_count, depth, out_cols), bf16),
            pltpu.VMEM((heads, tok, 2 * HD), f32),
            pltpu.VMEM((heads, tok, HD), f32),
            pltpu.VMEM((tok, cols), bf16),
            pltpu.VMEM((chips, chunks, tok, width), bf16),
            pltpu.VMEM((chips, chunks, tok, width), bf16),
            pltpu.VMEM((chips, chunks, tok, width), bf16),
            pltpu.VMEM((chips, chunks, tok, width), bf16),
            pltpu.VMEM((chunks, tok, width), f32),
            dma((4,)),
            dma((tp_count,)),
            dma((slots, 4)),
            dma((slots, 4)),
            dma((slots, 4)),
            dma((chips, chunks)),
            dma((chips, chunks)),
            dma((chips, chunks)),
            dma((chips, chunks)),
        ],
        compiler_params=pltpu.CompilerParams(
            collective_id=0, has_side_effects=True, vmem_limit_bytes=60 * 1024 * 1024
        ),
    )(block_mask, queries, keys, values, w_out)


def solution(mesh):
    return jax.shard_map(
        functools.partial(shards, mesh.shape["ctx"], mesh.shape["tp"]),
        mesh=mesh,
        in_specs=(P("ctx", "tp"), P("ctx", "tp"), P("ctx", "tp"), P(), P("tp", None)),
        out_specs=P("ctx", "tp"),
        check_vma=False,
    )
```

```python
import functools
import math

import jax
import jax.numpy as jnp
from jax import lax
from jax.experimental import pallas as pl
from jax.experimental.pallas import tpu as pltpu
from jax.sharding import PartitionSpec as P

HD = 128
BLK = 128
MESH = pl.DeviceIdType.MESH
K, V = 0, 1
OUTER_FIRST, ROW_FIRST = 0, 1


def kernel(
    reach, count, tp_count, chunks,
    mask_ref, q_ref, k_ref, v_ref, w_ref, near_ref, far_ref,
    kv, w_vm, acc, peak, att, stage_p, recv_p, stage_y, final,
    kv_local, w_local, own_send, relay_send, kv_recv, p_send, p_recv, y_send, y_recv, near_sem,
):
    tok, cols = q_ref.shape
    heads = cols // HD
    per = tok // BLK
    chips = tp_count // 2
    out_cols = near_ref.shape[1]
    width = out_cols // chunks
    ctx = lax.axis_index("ctx")
    t = lax.axis_index("tp")
    inner = lax.rem(ctx, reach)
    core = lax.rem(t, 2)
    chip = t // 2
    partner = chip * 2 + 1 - core

    def tp_of(jy, which):
        return lax.rem(chip + jy, chips) * 2 + which

    def each_peer(fn):
        if reach == 2:
            fn(1)
        elif reach > 2:
            def step(j, carry):
                fn(j)
                return carry
            lax.fori_loop(1, reach, step, 0)

    def row_peer(j):
        return ctx - inner + lax.rem(inner + j, reach)

    def inside(c):
        return jnp.logical_and(c >= 0, c < count)

    part_rows = tok // 2

    def part_of(half, kind):
        return (k_ref, v_ref)[kind].at[half * part_rows:(half + 1) * part_rows, :]

    own = [
        pltpu.make_async_copy(
            part_of(half, kind), kv.at[reach, half * 2 + kind], kv_local.at[half * 2 + kind]
        )
        for half in (0, 1) for kind in (K, V)
    ]
    weights = [
        pltpu.make_async_copy(
            w_ref.at[:, s * out_cols:(s + 1) * out_cols], w_vm.at[s], w_local.at[s]
        )
        for s in range(tp_count)
    ]
    for copy in own:
        copy.start()

    barrier = pltpu.get_barrier_semaphore()

    def greet(c, tt):
        pl.semaphore_signal(barrier, inc=1, device_id=(c, tt), device_id_type=MESH)

    each_peer(lambda j: greet(row_peer(j), t))
    for away in (-reach, reach):
        @pl.when(inside(ctx + away))
        def _(away=away):
            greet(ctx + away, t)
    greet(ctx, partner)
    for jy in range(1, chips):
        greet(ctx, tp_of(jy, core))
    outer_count = inside(ctx - reach).astype(jnp.int32) + inside(ctx + reach).astype(jnp.int32)
    pl.semaphore_wait(barrier, reach - 1 + 1 + chips - 1 + outer_count)

    class Pair:
        def __init__(self, make):
            self.copies = [make(K), make(V)]

        def start(self):
            for copy in self.copies:
                copy.start()

        def wait_send(self):
            for copy in self.copies:
                copy.wait_send()

        def wait_recv(self):
            for copy in self.copies:
                copy.wait_recv()

    def own_copy(dest, half):
        return Pair(lambda kind: pltpu.make_async_remote_copy(
            src_ref=part_of(half, kind),
            dst_ref=kv.at[ctx - dest + reach, half * 2 + kind],
            send_sem=own_send.at[dest - ctx + reach, half * 2 + kind],
            recv_sem=kv_recv.at[ctx - dest + reach, half * 2 + kind],
            device_id=(dest, t),
            device_id_type=MESH,
        ))

    def outer(fn):
        for away in (-reach, reach):
            @pl.when(inside(ctx + away))
            def _(away=away):
                fn(ctx + away)

    each_peer(lambda j: own_copy(row_peer(j), ROW_FIRST).start())
    outer(lambda dest: own_copy(dest, OUTER_FIRST).start())
    each_peer(lambda j: own_copy(row_peer(j), OUTER_FIRST).start())
    outer(lambda dest: own_copy(dest, ROW_FIRST).start())
    for copy in weights:
        copy.start()

    def wait_piece(src, half):
        slot = src - ctx + reach
        Pair(lambda kind: pltpu.make_async_remote_copy(
            src_ref=kv.at[slot, half * 2 + kind],
            dst_ref=kv.at[slot, half * 2 + kind],
            send_sem=own_send.at[slot, half * 2 + kind],
            recv_sem=kv_recv.at[slot, half * 2 + kind],
            device_id=(ctx, partner),
            device_id_type=MESH,
        )).wait_recv()

    def attend(src, halves, first=False):
        slot = src - ctx + reach
        factor = jnp.float32(HD ** (-0.5) * math.log2(math.e))
        half_blocks = per // 2
        blocks = [half * half_blocks + b for half in halves for b in range(half_blocks)]
        span = len(blocks) * BLK
        bias_rows = []
        for a in range(per):
            parts = []
            for b in blocks:
                flag = mask_ref[ctx * per + a, src * per + b]
                value = jnp.where(flag > 0, jnp.float32(0.0), jnp.float32(-1e30))
                parts.append(jnp.full((1, BLK), value, jnp.float32))
            bias_rows.append(jnp.concatenate(parts, axis=1))
        ones = jnp.ones((span, HD), jnp.bfloat16)
        for h in range(heads):
            lanes = slice(h * HD, (h + 1) * HD)
            key = jnp.concatenate([kv[slot, half * 2 + K, :, lanes] for half in halves], axis=0)
            value = jnp.concatenate([kv[slot, half * 2 + V, :, lanes] for half in halves], axis=0)
            raw = lax.dot_general(
                q_ref[:, lanes], key, (((1,), (1,)), ((), ())),
                preferred_element_type=jnp.float32,
            )
            weights_of, fades = [], []
            for a in range(per):
                rows = slice(a * BLK, (a + 1) * BLK)
                scores = raw[rows] + bias_rows[a]
                top = jnp.broadcast_to(jnp.max(scores, axis=1, keepdims=True), (BLK, HD))
                if not first:
                    before = peak[h, rows, :]
                    top = jnp.maximum(before, top)
                    fades.append(jnp.exp2((before - top) * factor))
                peak[h, rows, :] = top
                wide_top = jnp.concatenate([top] * len(blocks), axis=1)
                weights_of.append(jnp.exp2((scores - wide_top) * factor).astype(jnp.bfloat16))
            product = jnp.dot(
                jnp.concatenate(weights_of, axis=0),
                jnp.concatenate([value, ones], axis=1),
                preferred_element_type=jnp.float32,
            )
            if not first:
                fade = jnp.concatenate(fades, axis=0)
                product = product + acc[h] * jnp.concatenate([fade, fade], axis=1)
            acc[h] = product

    for copy in own:
        copy.wait()
    attend(ctx, (0, 1), True)

    def row_first_relay(j):
        peer = row_peer(j)
        dest = jnp.where(peer > ctx, ctx + reach, ctx - reach)
        return inside(dest), Pair(lambda kind: pltpu.make_async_remote_copy(
            src_ref=kv.at[peer - ctx + reach, ROW_FIRST * 2 + kind],
            dst_ref=kv.at[peer - dest + reach, ROW_FIRST * 2 + kind],
            send_sem=relay_send.at[peer - ctx + reach, ROW_FIRST * 2 + kind],
            recv_sem=kv_recv.at[peer - dest + reach, ROW_FIRST * 2 + kind],
            device_id=(dest, t),
            device_id_type=MESH,
        ))

    def outer_first_relay(j):
        peer = row_peer(j)
        src = jnp.where(peer < ctx, ctx - reach, ctx + reach)
        return inside(src), Pair(lambda kind: pltpu.make_async_remote_copy(
            src_ref=kv.at[src - ctx + reach, OUTER_FIRST * 2 + kind],
            dst_ref=kv.at[src - peer + reach, OUTER_FIRST * 2 + kind],
            send_sem=relay_send.at[peer - ctx + reach, OUTER_FIRST * 2 + kind],
            recv_sem=kv_recv.at[src - peer + reach, OUTER_FIRST * 2 + kind],
            device_id=(peer, t),
            device_id_type=MESH,
        ))

    def start_relay(make, j):
        valid, copy = make(j)

        @pl.when(valid)
        def _():
            copy.start()

    def end_relay(make, j):
        valid, copy = make(j)

        @pl.when(valid)
        def _():
            copy.wait_send()

    def pass_row(j):
        wait_piece(row_peer(j), ROW_FIRST)
        start_relay(row_first_relay, j)

    each_peer(pass_row)
    outer(lambda src: wait_piece(src, OUTER_FIRST))
    each_peer(lambda j: start_relay(outer_first_relay, j))
    each_peer(lambda j: attend(row_peer(j), (ROW_FIRST,)))
    outer(lambda src: attend(src, (OUTER_FIRST,)))

    def take_row(j):
        wait_piece(row_peer(j), OUTER_FIRST)
        attend(row_peer(j), (OUTER_FIRST,))

    each_peer(take_row)

    def take_outer(src):
        wait_piece(src, ROW_FIRST)
        attend(src, (ROW_FIRST,))

    outer(take_outer)
    for copy in weights:
        copy.wait()

    def take_diagonal(j):
        peer = row_peer(j)
        src = jnp.where(peer > ctx, peer - reach, peer + reach)

        @pl.when(inside(src))
        def _():
            wait_piece(src, OUTER_FIRST)
            wait_piece(src, ROW_FIRST)
            attend(src, (0, 1))

    each_peer(take_diagonal)

    for h in range(heads):
        lanes = slice(h * HD, (h + 1) * HD)
        att[:, lanes] = (acc[h, :, :HD] * (1.0 / acc[h, :, HD:])).astype(jnp.bfloat16)

    def project(slab, k):
        return jnp.dot(
            att[...], w_vm[slab, :, k * width:(k + 1) * width],
            preferred_element_type=jnp.float32,
        )

    def partner_copy(jy, k):
        return pltpu.make_async_remote_copy(
            src_ref=stage_p.at[jy, k],
            dst_ref=recv_p.at[jy, k],
            send_sem=p_send.at[jy, k],
            recv_sem=p_recv.at[jy, k],
            device_id=(ctx, partner),
            device_id_type=MESH,
        )

    def chip_copy(jy, k):
        return pltpu.make_async_remote_copy(
            src_ref=stage_y.at[jy, k],
            dst_ref=far_ref.at[chips - jy - 1, :, k * width:(k + 1) * width],
            send_sem=y_send.at[jy, k],
            recv_sem=y_recv.at[chips - jy, k],
            device_id=(ctx, tp_of(jy, core)),
            device_id_type=MESH,
        )

    def near_copy(k):
        return pltpu.make_async_copy(
            final.at[k], near_ref.at[:, k * width:(k + 1) * width], near_sem.at[k]
        )

    pending = []

    def push(copy):
        while pending:
            pending.pop().start()
        if copy is not None:
            pending.append(copy)

    for jy in range(1, chips):
        there, here = tp_of(jy, 1 - core), tp_of(jy, core)
        for step in range(chunks + 1):
            if step < chunks:
                @pl.when(t >= 0)
                def _():
                    stage_p[jy, step] = project(there, step).astype(jnp.bfloat16)
                push(partner_copy(jy, step))
            if step > 0:
                k = step - 1
                if step == chunks:
                    push(None)
                partner_copy(jy, k).wait_recv()

                @pl.when(t >= 0)
                def _():
                    mine = project(here, k) + recv_p[jy, k].astype(jnp.float32)
                    stage_y[jy, k] = mine.astype(jnp.bfloat16)
                push(chip_copy(jy, k))
    for k in range(chunks):
        stage_p[0, k] = project(tp_of(0, 1 - core), k).astype(jnp.bfloat16)
        push(partner_copy(0, k))
    for k in range(chunks):
        mine = project(tp_of(0, core), k)
        push(None)
        partner_copy(0, k).wait_recv()
        final[k] = mine + recv_p[0, k].astype(jnp.float32)
        push(near_copy(k))
    push(None)
    for k in range(chunks):
        for jy in range(1, chips):
            chip_copy(chips - jy, k).wait_recv()
        near_copy(k).wait()

    each_peer(lambda j: own_copy(row_peer(j), ROW_FIRST).wait_send())
    each_peer(lambda j: own_copy(row_peer(j), OUTER_FIRST).wait_send())
    outer(lambda dest: own_copy(dest, OUTER_FIRST).wait_send())
    outer(lambda dest: own_copy(dest, ROW_FIRST).wait_send())
    each_peer(lambda j: end_relay(row_first_relay, j))
    each_peer(lambda j: end_relay(outer_first_relay, j))
    for jy in range(chips):
        for k in range(chunks):
            partner_copy(jy, k).wait_send()
    for jy in range(1, chips):
        for k in range(chunks):
            chip_copy(jy, k).wait_send()


def shards(count, tp_count, queries, keys, values, block_mask, w_out):
    tok, cols = queries.shape
    heads = cols // HD
    reach = count // 4
    chips = tp_count // 2
    depth, wide = w_out.shape
    out_cols = wide // tp_count
    chunks = max(1, out_cols // 256)
    width = out_cols // chunks
    bf16, f32 = jnp.bfloat16, jnp.float32
    dma = pltpu.SemaphoreType.DMA
    slots = 2 * reach + 1
    near, far = pl.pallas_call(
        functools.partial(kernel, reach, count, tp_count, chunks),
        out_shape=[
            jax.ShapeDtypeStruct((tok, out_cols), f32),
            jax.ShapeDtypeStruct((chips - 1, tok, out_cols), bf16),
        ],
        in_specs=[
            pl.BlockSpec(memory_space=pltpu.SMEM),
            pl.BlockSpec(memory_space=pltpu.VMEM),
            pl.BlockSpec(memory_space=pl.ANY),
            pl.BlockSpec(memory_space=pl.ANY),
            pl.BlockSpec(memory_space=pl.ANY),
        ],
        out_specs=[pl.BlockSpec(memory_space=pl.ANY)] * 2,
        scratch_shapes=[
            pltpu.VMEM((slots, 4, tok // 2, cols), bf16),
            pltpu.VMEM((tp_count, depth, out_cols), bf16),
            pltpu.VMEM((heads, tok, 2 * HD), f32),
            pltpu.VMEM((heads, tok, HD), f32),
            pltpu.VMEM((tok, cols), bf16),
            pltpu.VMEM((chips, chunks, tok, width), bf16),
            pltpu.VMEM((chips, chunks, tok, width), bf16),
            pltpu.VMEM((chips, chunks, tok, width), bf16),
            pltpu.VMEM((chunks, tok, width), f32),
            dma((4,)),
            dma((tp_count,)),
            dma((slots, 4)),
            dma((slots, 4)),
            dma((slots, 4)),
            dma((chips, chunks)),
            dma((chips, chunks)),
            dma((chips, chunks)),
            dma((chips, chunks)),
            dma((chunks,)),
        ],
        compiler_params=pltpu.CompilerParams(
            collective_id=0, has_side_effects=True, vmem_limit_bytes=60 * 1024 * 1024
        ),
    )(block_mask, queries, keys, values, w_out)
    for other in range(chips - 1):
        near = near + far[other].astype(f32)
    return near.astype(bf16)


def solution(mesh):
    return jax.shard_map(
        functools.partial(shards, mesh.shape["ctx"], mesh.shape["tp"]),
        mesh=mesh,
        in_specs=(P("ctx", "tp"), P("ctx", "tp"), P("ctx", "tp"), P(), P("tp", None)),
        out_specs=P("ctx", "tp"),
        check_vma=False,
    )
```
